32 devices in a mesh: depth: 2 (over x), gx: 8 (over z, y), gy: 2 (over core).
Axes of the slice: x: 2, y: 2, z: 4, core: 2. Of those that a mesh axis runs over, the one named last changes fastest.
Arguments:
- operator: bfloat16 [2, 8, 2, 1536, 1536], P('depth', 'gx', 'gy')
- sources: bfloat16 [2, 8, 2, 768, 1024], P('depth', 'gx', 'gy'), may hold values from -6 to 6
Outputs:
- solution: bfloat16 [2, 8, 2, 768, 1024], P('depth', 'gx', 'gy')
The draws below stay inside these ranges and needn't reach their ends.
All inputs are finite; a program needn't handle non-finite values.
Results may differ from the reference program's by a relative error of at most 0.017.
Values may be sent and summed in bfloat16 or wider, within the bound.
No kernel may reach another device: no remote copies, remote signals or barrier semaphores. Data moves between devices by JAX's collectives and lax.ppermute only.
A program may use at most 64 MiB of HBM per device.

```python
import math
import jax
import jax.numpy as jnp

TRACE = 256
INNER = 768
ORDER = 1536
COLS = 1024
N_DEPTH = 2
N_GX = 8
N_GY = 2


def draw_operator(key, part):
    total = float(N_DEPTH + N_GX + N_GY)
    column = jnp.arange(ORDER)
    block = column // TRACE
    gains = jnp.array([N_GX / total, N_GY / total, N_DEPTH / total], jnp.float32)
    trace_scale = jnp.sqrt(gains[jnp.minimum(block, 2)] / TRACE)
    source_scale = jnp.float32(math.sqrt(0.5 / INNER))
    scales = jnp.where(column < 3 * TRACE, trace_scale, source_scale).astype(jnp.float32)
    shape = (N_DEPTH, N_GX, N_GY, ORDER, ORDER)
    values = jnp.clip(jax.random.normal(key, shape, jnp.float32), -4.0, 4.0)
    return (values * scales).astype(jnp.bfloat16)


def steps_of(rng, shape, pieces, least, largest):
    def one(axis_at, parts):
        heights = jax.random.uniform(jax.random.fold_in(jax.random.fold_in(rng, 6), axis_at), (parts,), jnp.float32, least / len(pieces), largest / len(pieces))
        return jnp.repeat(jnp.exp(heights), shape[axis_at] // parts).reshape((-1,) + (1,) * (len(shape) - axis_at - 1))

    level = one(*pieces[0])
    for cut in pieces[1:]:
        level = level * one(*cut)
    return level


def gaussian(own_key, shape, scale, limit, split=(), kind=jnp.bfloat16):
    values = scale * jax.random.normal(own_key, shape, jnp.float32)
    if split:
        values = values * steps_of(own_key, shape, split, -0.22, 0.18)
    return jnp.clip(values, -limit, limit).astype(kind)


def setup_inputs(seed: int = 0) -> dict:
    key_of = jax.random.split(jax.random.key(seed), 3)
    return {
        "operator": draw_operator(jax.random.fold_in(key_of[2], 71), 0),
        "sources": gaussian(key_of[1], (N_DEPTH, N_GX, N_GY, INNER, COLS), 1.0, 6.0, ((0, 2), (1, 8), (2, 2))),
    }


def reference(operator, sources):
    zero_trace = jnp.zeros((TRACE, COLS), jnp.bfloat16)
    results = {}
    solved = []
    for dd in range(N_DEPTH):
        plane = []
        for ii in range(N_GX):
            column = []
            for jj in range(N_GY):
                x_part = results[(dd, ii - 1, jj)][0:TRACE] if ii > 0 else zero_trace
                y_part = results[(dd, ii, jj - 1)][TRACE:2 * TRACE] if jj > 0 else zero_trace
                z_part = results[(dd - 1, ii, jj)][2 * TRACE:3 * TRACE] if dd > 0 else zero_trace
                stacked = jnp.concatenate([x_part, y_part, z_part, sources[dd, ii, jj]], axis=0)
                result = jnp.dot(operator[dd, ii, jj], stacked, preferred_element_type=jnp.float32).astype(jnp.bfloat16)
                results[(dd, ii, jj)] = result
                column.append(result[3 * TRACE:])
            plane.append(jnp.stack(column, axis=0))
        solved.append(jnp.stack(plane, axis=0))
    return jnp.stack(solved, axis=0)
```

```python
import functools
import jax
import jax.numpy as jnp
from jax import lax
from jax.experimental import pallas as pl
from jax.experimental.pallas import tpu as pltpu
from jax.sharding import PartitionSpec as P

STREAMS = 1
WAVES = 2
VMEM = pl.BlockSpec(memory_space=pltpu.VMEM)
SMEM = pl.BlockSpec(memory_space=pltpu.SMEM)
ANY = pl.BlockSpec(memory_space=pl.ANY)
AXES = ("depth", "gx", "gy")
f32 = jnp.float32
bf16 = jnp.bfloat16


def dot(a, b):
    return jnp.dot(a, b, preferred_element_type=f32)


def params(mib):
    return pltpu.CompilerParams(vmem_limit_bytes=mib << 20)


def cost(m, k, n):
    return pl.CostEstimate(flops=2 * m * k * n, bytes_accessed=2 * (m * k + k * n + m * n), transcendentals=0)


def route(sizes, axis, first, last):
    nd, nx, ny = sizes
    pairs = []
    for d in range(nd):
        for i in range(nx):
            for j in range(ny):
                at = [d, i, j]
                to = list(at)
                to[axis] += 1
                if to[axis] < sizes[axis] and first <= d + i + j <= last:
                    pairs.append(((d * nx + i) * ny + j, (to[0] * nx + to[1]) * ny + to[2]))
    return pairs


def source_kernel(rows, op_ref, src_ref, out_ref):
    out_ref[...] = dot(op_ref[:rows, rows:], src_ref[...])


def tick_kernel(tick, waves, trace, base, width, level_ref, op_ref, s_ref, xi, yi, zi, x_ref, y_ref, z_ref):
    piece = tick - level_ref[0]

    @pl.when(jnp.logical_and(piece >= 0, piece < waves))
    def _():
        local = 0 if waves == 1 else pl.multiple_of(piece * width, 128)
        for n, ref in enumerate((x_ref, y_ref, z_ref)):
            rows = slice(n * trace, (n + 1) * trace)
            total = s_ref[rows, pl.ds(base + local, width)]
            for m, part in enumerate((xi, yi, zi)):
                total += dot(op_ref[rows, m * trace : (m + 1) * trace], part[...])
            ref[...] = total.astype(bf16)


def solve_kernel(trace, base, width, op_ref, src_ref, xi, yi, zi, out_in, out_ref, buf, sem):
    del out_in
    rows = 3 * trace
    total = dot(op_ref[rows:, rows:], src_ref[:, base : base + width])
    for m, part in enumerate((xi, yi, zi)):
        total += dot(op_ref[rows:, m * trace : (m + 1) * trace], part[...])
    buf[...] = total.astype(bf16)
    copy = pltpu.make_async_copy(buf, out_ref.at[:, pl.ds(base, width)], sem)
    copy.start()
    copy.wait()


def empty_kernel(*refs):
    del refs


def shards(sizes, operator, sources):
    op = operator[0, 0, 0]
    src = sources[0, 0, 0]
    inner, columns = src.shape
    trace = (op.shape[0] - inner) // 3
    rows = 3 * trace
    width = columns // (STREAMS * WAVES)
    top = sum(sizes) - 3
    level = (lax.axis_index("depth") + lax.axis_index("gx") + lax.axis_index("gy")).astype(jnp.int32).reshape(1)
    trace_type = jax.ShapeDtypeStruct((trace, width), bf16)
    group = WAVES * width
    source = pl.pallas_call(
        functools.partial(source_kernel, rows),
        out_shape=jax.ShapeDtypeStruct((rows, columns), f32),
        in_specs=[VMEM, VMEM],
        out_specs=VMEM,
        compiler_params=params(8),
        cost_estimate=cost(rows, inner, columns),
        name="source",
    )(op, src)
    out = pl.pallas_call(
        empty_kernel,
        out_shape=jax.ShapeDtypeStruct((inner, columns), bf16),
        out_specs=ANY,
        compiler_params=params(1),
        name="room",
    )()
    zero = jnp.zeros((trace, width), bf16)
    held = [[zero, zero, zero] for _ in range(STREAMS)]
    kept = [[[zero, zero, zero] for _ in range(WAVES)] for _ in range(STREAMS)]

    def solve(out, n, wave):
        base = n * group + wave * width
        return pl.pallas_call(
            functools.partial(solve_kernel, trace, base, width),
            out_shape=jax.ShapeDtypeStruct((inner, columns), bf16),
            in_specs=[VMEM] * 5 + [ANY],
            out_specs=ANY,
            scratch_shapes=[pltpu.VMEM((inner, width), bf16), pltpu.SemaphoreType.DMA],
            input_output_aliases={5: 0},
            compiler_params=params(8),
            cost_estimate=cost(inner, rows + inner, width),
            name="solve",
        )(op, src, *kept[n][wave], out)

    for tick in range(top + WAVES):
        for n in range(STREAMS):
            for wave in range(WAVES):
                if 0 < tick - wave <= top:
                    mine = level[0] == tick - wave
                    kept[n][wave] = [jnp.where(mine, a, b) for a, b in zip(held[n], kept[n][wave])]
            if tick >= top:
                out = solve(out, n, tick - top)
            if tick == top + WAVES - 1:
                continue
            sent = pl.pallas_call(
                functools.partial(tick_kernel, tick, WAVES, trace, n * group, width),
                out_shape=[trace_type] * 3,
                in_specs=[SMEM] + [VMEM] * 5,
                out_specs=[VMEM] * 3,
                compiler_params=params(8),
                cost_estimate=cost(rows, rows, width),
                name="tick",
            )(level, op, source, *held[n])
            held[n] = [
                lax.ppermute(block, AXES, route(sizes, axis, tick - WAVES + 1, tick))
                for block, axis in zip(sent, (1, 2, 0))
            ]
    return out[None, None, None]


def solution(mesh):
    spec = P("depth", "gx", "gy", None, None)
    sizes = tuple(mesh.shape[a] for a in AXES)
    return jax.shard_map(
        functools.partial(shards, sizes), mesh=mesh, in_specs=(spec, spec), out_specs=spec, check_vma=False
    )
```

```python
import functools
import jax
import jax.numpy as jnp
from jax import lax
from jax.experimental import pallas as pl
from jax.experimental.pallas import tpu as pltpu
from jax.sharding import PartitionSpec as P

STREAMS = 4
REPEAT = 4
VMEM = pl.BlockSpec(memory_space=pltpu.VMEM)
SMEM = pl.BlockSpec(memory_space=pltpu.SMEM)
HBM = pl.BlockSpec(memory_space=pltpu.HBM)
AXES = ("depth", "gx", "gy")
f32 = jnp.float32
bf16 = jnp.bfloat16


def dot(a, b):
    return jnp.dot(a, b, preferred_element_type=f32)


def shaped(shape, dtype=bf16):
    return jax.ShapeDtypeStruct(shape, dtype)


def call(kernel, ins, outs, out_specs, mib, flops, nbytes, scratch=(), aliases=None):
    return pl.pallas_call(
        kernel,
        out_shape=outs,
        in_specs=ins,
        out_specs=out_specs,
        scratch_shapes=list(scratch),
        input_output_aliases=aliases or {},
        compiler_params=pltpu.CompilerParams(vmem_limit_bytes=mib << 20),
        cost_estimate=pl.CostEstimate(flops=flops, bytes_accessed=nbytes, transcendentals=0),
    )


def route(sizes, axis, tick):
    nd, nx, ny = sizes
    pairs = []
    for d in range(nd):
        for i in range(nx):
            for j in range(ny):
                group = j // 2
                at, to = [d, i, group], [d, i, group]
                to[axis] += 1
                if to[axis] < (nd, nx, ny // 2)[axis] and (sum(at) - tick) % (REPEAT if axis == 1 else 8) == 0:
                    end = (to[0] * nx + to[1]) * ny + 2 * to[2] + j % 2
                    pairs.append(((d * nx + i) * ny + j, end))
    return pairs


def fetch_kernel(rows, op_ref, t_ref):
    t_ref[...] = op_ref[:rows, :rows]


def give_kernel(rows, half, parity_ref, op_ref, src_ref, give_ref):
    other = pl.ds(pl.multiple_of((1 - parity_ref[0]) * half, 128), half)
    step = rows // 3

    def body(n, _):
        part = pl.ds(pl.multiple_of(n * step, step), step)
        give_ref[part, :] = dot(op_ref[part, rows:], src_ref[:, other]).astype(bf16)
        return 0

    lax.fori_loop(0, 3, body, 0)


def own_kernel(half, parity_ref, op_ref, src_ref, t_ref, got_ref, both_ref, s_ref):
    trows = t_ref.shape[0]
    step = trows // 3
    mine = pl.ds(pl.multiple_of(parity_ref[0] * half, 128), half)

    def body(n, _):
        rows = pl.ds(pl.multiple_of(n * step, step), step)
        s_ref[rows, :] = dot(op_ref[rows, trows:], src_ref[:, mine])
        both_ref[parity_ref[0], rows, :] = t_ref[rows, :]
        both_ref[1 - parity_ref[0], rows, :] = got_ref[rows, :]
        return 0

    lax.fori_loop(0, 3, body, 0)


def pair_sources(parity_ref, s_ref, given_ref, rows, columns):
    own, given = s_ref[rows, columns], given_ref[rows, columns].astype(f32)
    even = parity_ref[0] == 0
    return jnp.where(even, own, given), jnp.where(even, given, own)


def lower_side(op, rows, trace, total, parts):
    for n, part in enumerate(parts):
        if part is not None:
            total += dot(op[rows, n * trace : (n + 1) * trace], part)
    return total


def halves(ref, trace):
    return (None, None) if ref is None else (ref[:trace, :], ref[trace:, :])


def paired(ref, trace, slot):
    if ref is None:
        return None, None
    at = 2 * slot * trace
    return ref[at : at + trace, :], ref[at + trace : at + 2 * trace, :]


def tick_kernel(tick, trace, columns, slot, moving, has_row, level_ref, parity_ref, both_ref, s_ref, given_ref, turn_ref, *refs):
    del turn_ref
    refs = list(refs)
    x_in = refs.pop(0) if moving else None
    z_in = refs.pop(0) if moving else None
    y_in = refs.pop(0) if moving and has_row else None
    first = refs.pop(0) if slot else None
    x_out, z_out, mid_out = refs[:3]

    @pl.when(level_ref[0] == tick)
    def _():
        xa, xb = halves(x_in, trace)
        za, zb = paired(z_in, trace, slot)
        ya = None if y_in is None else y_in[...]
        sa, sb = pair_sources(parity_ref, s_ref, given_ref, slice(0, 3 * trace), columns)
        every = slice(0, 3 * trace)
        a = lower_side(both_ref.at[0], every, trace, sa, (xa, ya, za)).astype(bf16)
        mid = a[trace : 2 * trace]
        b = lower_side(both_ref.at[1], every, trace, sb, (xb, None, zb))
        b = lower_side(both_ref.at[1], every, trace, b, (None, mid, None)).astype(bf16)
        x_out[:trace, :] = a[:trace]
        x_out[trace:, :] = b[:trace]
        if slot:
            z_out[: 2 * trace, :] = first[...]
        z_out[2 * slot * trace : (2 * slot + 1) * trace, :] = a[2 * trace :]
        z_out[(2 * slot + 1) * trace : (2 * slot + 2) * trace, :] = b[2 * trace :]
        mid_out[...] = mid
        if has_row:
            refs[3][...] = b[trace : 2 * trace]


def last_kernel(top, trace, width, base, has_row, level_ref, parity_ref, both_ref, s_ref, given_ref, turn_ref, *refs):
    del turn_ref
    refs = list(refs)
    own_ref, give_ref = refs[-2:]
    even = parity_ref[0] == 0
    zero = jnp.zeros((trace, width), bf16)

    def put(n, slot, a, b):
        rows = slice(n * trace, (n + 1) * trace)
        cols = slice(slot * width, (slot + 1) * width)
        own_ref[rows, cols] = jnp.where(even, a, b)
        give_ref[rows, cols] = jnp.where(even, b, a)

    for tick in range(top + 1):
        z_in = refs.pop(0) if tick else None
        xs = [refs.pop(0) for _ in range(2)] if tick else [None] * 2
        ys = [refs.pop(0) for _ in range(2)] if tick and has_row else [None] * 2
        mids = [refs.pop(0) for _ in range(2)] if tick < top else [None] * 2

        @pl.when(level_ref[0] == tick)
        def _():
            for slot in range(2):
                xa, xb = halves(xs[slot], trace)
                za, zb = paired(z_in, trace, slot)
                ya = None if ys[slot] is None else ys[slot][...]
                if mids[slot] is None:
                    rows = slice(trace, 2 * trace)
                    start = base + slot * width
                    sa, _ = pair_sources(parity_ref, s_ref, given_ref, rows, slice(start, start + width))
                    yb = lower_side(both_ref.at[0], rows, trace, sa, (xa, ya, za)).astype(bf16)
                else:
                    yb = mids[slot][...]
                put(0, slot, zero if xa is None else xa, zero if xb is None else xb)
                put(1, slot, zero if ya is None else ya, yb)
                put(2, slot, zero if za is None else za, zero if zb is None else zb)


def solve_kernel(rows, half, base, side, parity_ref, op_ref, src_ref, in_ref, out_in, out_ref, token_ref, buf, sem):
    del out_in
    width = buf.shape[1]
    at = parity_ref[0] if side == 0 else 1 - parity_ref[0]
    columns = pl.ds(pl.multiple_of(at * half + base, 128), width)
    step = buf.shape[0] // 3

    def body(n, _):
        local = pl.ds(pl.multiple_of(n * step, step), step)
        below = pl.ds(pl.multiple_of(rows + n * step, step), step)
        total = dot(op_ref[below, rows:], src_ref[:, columns])
        total += dot(op_ref[below, :rows], in_ref[...])
        buf[local, :] = total.astype(bf16)
        return 0

    lax.fori_loop(0, 3, body, 0)
    copy = pltpu.make_async_copy(buf, out_ref.at[:, columns], sem)
    copy.start()
    token_ref[...] = jnp.zeros(token_ref.shape, token_ref.dtype)
    copy.wait()


def room_kernel(out_ref):
    del out_ref


def shards(sizes, operator, sources):
    op = operator[0, 0, 0]
    src = sources[0, 0, 0]
    inner, columns = src.shape
    trace = (op.shape[0] - inner) // 3
    rows = 3 * trace
    half = columns // 2
    width = half // STREAMS
    nd, nx, ny = sizes
    top = nd + nx + ny // 2 - 3
    has_row = ny > 2
    row = lax.axis_index("gy")
    level = lax.axis_index("depth") + lax.axis_index("gx") + (row >> 1)
    level = level.astype(jnp.int32).reshape(1)
    parity = (row & 1).astype(jnp.int32).reshape(1)
    op, src, level, parity = lax.optimization_barrier((op, src, level, parity))
    swap = [(j, j ^ 1) for j in range(ny)]

    t = call(functools.partial(fetch_kernel, rows), [VMEM], shaped((rows, rows)), VMEM, 1, 0, 0)(op)
    got = lax.ppermute(t, "gy", swap)
    give = call(
        functools.partial(give_kernel, rows, half), [SMEM, VMEM, VMEM], shaped((rows, half)), VMEM, 4, 0, 0
    )(parity, op, src)
    given = lax.ppermute(give, "gy", swap)
    both, s = call(
        functools.partial(own_kernel, half), [SMEM] + [VMEM] * 4,
        [shaped((2, rows, rows)), shaped((rows, half), f32)], [VMEM] * 2, 4, 0, 0,
    )(parity, op, src, t, got)
    out = call(room_kernel, [], shaped((inner, columns)), HBM, 1, 0, 0)()

    turn = given
    xs = [[] for _ in range(STREAMS)]
    ys = [[] for _ in range(STREAMS)]
    zs = [[] for _ in range(STREAMS // 2)]
    mids = [[] for _ in range(STREAMS)]
    for tick in range(top):
        for n in range(STREAMS):
            slot = n % 2
            cols = slice(n * width, (n + 1) * width)
            outs = [shaped((2 * trace, width)), shaped((2 * (slot + 1) * trace, width)), shaped((trace, width))]
            outs += [shaped((trace, width))] * has_row
            ins = [turn]
            if tick:
                ins += [xs[n][-1], zs[n // 2][tick - 1]]
                ins += [ys[n][-1]] if has_row else []
            if slot:
                ins.append(pair)
            sent = call(
                functools.partial(tick_kernel, tick, trace, cols, slot, tick > 0, has_row),
                [SMEM] * 2 + [VMEM] * (3 + len(ins)), outs, [VMEM] * len(outs), 4, 0, 0,
            )(level, parity, both, s, given, *ins)
            pair, turn = sent[1:3]
            mids[n].append(turn)
            xs[n].append(lax.ppermute(sent[0], AXES, route(sizes, 1, tick)))
            if has_row:
                ys[n].append(lax.ppermute(sent[3], AXES, route(sizes, 2, tick)))
            if slot:
                zs[n // 2].append(lax.ppermute(pair, AXES, route(sizes, 0, tick)))
    for p in range(STREAMS // 2):
        ins = []
        for tick in range(top + 1):
            ins += [zs[p][tick - 1]] if tick else []
            for part in (xs, ys) if has_row else (xs,):
                ins += [part[2 * p + slot][tick - 1] for slot in range(2)] if tick else []
            ins += [mids[2 * p + slot][tick] for slot in range(2)] if tick < top else []
        base = 2 * p * width
        mine, other = call(
            functools.partial(last_kernel, top, trace, width, base, has_row),
            [SMEM] * 2 + [VMEM] * (4 + len(ins)), [shaped((rows, 2 * width))] * 2, [VMEM] * 2, 4, 0, 0,
        )(level, parity, both, s, given, turn, *ins)
        back = lax.ppermute(other, "gy", swap)
        for side, part in enumerate((mine, back)):
            out, turn = call(
                functools.partial(solve_kernel, rows, half, base, side), [SMEM] + [VMEM] * 3 + [HBM],
                [shaped((inner, columns)), shaped((8, 128), f32)], [HBM, VMEM], 4, 0, 0,
                scratch=[pltpu.VMEM((inner, 2 * width), bf16), pltpu.SemaphoreType.DMA], aliases={4: 0},
            )(parity, op, src, part, out)
    return out[None, None, None]


def solution(mesh):
    spec = P("depth", "gx", "gy", None, None)
    sizes = tuple(mesh.shape[a] for a in AXES)
    return jax.shard_map(
        functools.partial(shards, sizes), mesh=mesh, in_specs=(spec, spec), out_specs=spec, check_vma=False
    )
```

```python
import functools
import jax
import jax.numpy as jnp
from jax import lax
from jax.experimental import pallas as pl
from jax.experimental.pallas import tpu as pltpu
from jax.sharding import PartitionSpec as P

STREAMS = 4
BLOCKS = 2
REPEAT = (8, 4, 4)
VMEM = pl.BlockSpec(memory_space=pltpu.VMEM)
SMEM = pl.BlockSpec(memory_space=pltpu.SMEM)
HBM = pl.BlockSpec(memory_space=pltpu.HBM)
AXES = ("depth", "gx", "gy")
f32 = jnp.float32
bf16 = jnp.bfloat16


def dot(a, b):
    return jnp.dot(a, b, preferred_element_type=f32)


def shaped(shape, dtype=bf16):
    return jax.ShapeDtypeStruct(shape, dtype)


def call(kernel, ins, outs, out_specs, mib, flops, nbytes, scratch=(), aliases=None):
    return pl.pallas_call(
        kernel,
        out_shape=outs,
        in_specs=ins,
        out_specs=out_specs,
        scratch_shapes=list(scratch),
        input_output_aliases=aliases or {},
        compiler_params=pltpu.CompilerParams(vmem_limit_bytes=mib << 20),
        cost_estimate=pl.CostEstimate(flops=flops, bytes_accessed=nbytes, transcendentals=0),
    )


def route(sizes, axis, tick):
    nd, nx, ny = sizes
    pairs = []
    for d in range(nd):
        for i in range(nx):
            for j in range(ny):
                group = j // 2
                at, to = [d, i, group], [d, i, group]
                to[axis] += 1
                if to[axis] < (nd, nx, ny // 2)[axis] and (sum(at) - tick) % REPEAT[axis] == 0:
                    end = (to[0] * nx + to[1]) * ny + 2 * to[2] + j % 2
                    pairs.append(((d * nx + i) * ny + j, end))
    return pairs


def fetch_kernel(trace, op_ref, turn_ref, mid_ref, rest_ref):
    del turn_ref
    mid_ref[...] = op_ref[:, trace : 2 * trace]
    rest_ref[:, :trace] = op_ref[:, :trace]
    rest_ref[:, trace:] = op_ref[:, 2 * trace : 3 * trace]


def give_kernel(half, parity_ref, op_ref, src_ref, turn_ref, give_ref):
    del turn_ref
    columns = pl.ds(pl.multiple_of((1 - parity_ref[0]) * half, 128), half)
    rows = op_ref.shape[0]
    give_ref[...] = dot(op_ref[:, rows:], src_ref[:, columns]).astype(bf16)


def half_kernel(half, parity_ref, op_ref, src_ref, turn_ref, out_ref):
    del turn_ref
    columns = pl.ds(pl.multiple_of(parity_ref[0] * half, 128), half)
    rows = out_ref.shape[0]
    step = rows // 3

    def body(n, _):
        part = pl.ds(pl.multiple_of(n * step, step), step)
        out_ref[part, :] = dot(op_ref[part, rows:], src_ref[:, columns])
        return 0

    lax.fori_loop(0, 3, body, 0)


def both_kernel(parity_ref, op_ref, mid_ref, turn_ref, *refs):
    del turn_ref
    *rest, both_ref = refs
    trace = mid_ref.shape[1]
    own, other = parity_ref[0], 1 - parity_ref[0]
    both_ref[own, :, trace : 2 * trace] = op_ref[:, trace : 2 * trace]
    both_ref[other, :, trace : 2 * trace] = mid_ref[...]
    for rest_ref in rest:
        both_ref[own, :, :trace] = op_ref[:, :trace]
        both_ref[own, :, 2 * trace :] = op_ref[:, 2 * trace : 3 * trace]
        both_ref[other, :, :trace] = rest_ref[:, :trace]
        both_ref[other, :, 2 * trace :] = rest_ref[:, trace:]


def lower_kernel(rows, op_ref, src_ref, turn_ref, r_ref, token_ref):
    del turn_ref
    step = r_ref.shape[0] // 3
    token_ref[...] = jnp.zeros(token_ref.shape, token_ref.dtype)

    def body(n, _):
        part = pl.ds(pl.multiple_of(n * step, step), step)
        below = pl.ds(pl.multiple_of(rows + n * step, step), step)
        r_ref[part, :] = dot(op_ref[below, rows:], src_ref[...])
        return 0

    lax.fori_loop(0, 3, body, 0)


def pair_sources(parity_ref, s_ref, given_ref, rows, columns):
    own, given = s_ref[rows, columns], given_ref[rows, columns].astype(f32)
    even = parity_ref[0] == 0
    return jnp.where(even, own, given), jnp.where(even, given, own)


def lower_side(op, rows, trace, total, parts):
    for n, part in enumerate(parts):
        if part is not None:
            total += dot(op[rows, n * trace : (n + 1) * trace], part)
    return total


def halves(ref, trace):
    return (None, None) if ref is None else (ref[:trace, :], ref[trace:, :])


def paired(ref, trace, slot):
    if ref is None:
        return None, None
    at = 2 * slot * trace
    return ref[at : at + trace, :], ref[at + trace : at + 2 * trace, :]


def tick_kernel(tick, trace, columns, slot, moving, has_row, level_ref, parity_ref, both_ref, s_ref, given_ref, turn_ref, *refs):
    del turn_ref
    refs = list(refs)
    x_in = refs.pop(0) if moving else None
    z_in = refs.pop(0) if moving else None
    y_in = refs.pop(0) if moving and has_row else None
    x_out, mid_out = refs[:2]

    @pl.when(level_ref[0] == tick)
    def _():
        xa, xb = halves(x_in, trace)
        za, zb = paired(z_in, trace, slot)
        ya = None if y_in is None else y_in[...]
        upper = slice(0, 2 * trace)
        sa, sb = pair_sources(parity_ref, s_ref, given_ref, upper, columns)
        a = lower_side(both_ref.at[0], upper, trace, sa, (xa, ya, za)).astype(bf16)
        mid = a[trace:]
        wanted = slice(0, (1 + has_row) * trace)
        b = lower_side(both_ref.at[1], wanted, trace, sb[wanted], (xb, None, zb))
        b = lower_side(both_ref.at[1], wanted, trace, b, (None, mid, None)).astype(bf16)
        x_out[:trace, :] = a[:trace]
        x_out[trace:, :] = b[:trace]
        mid_out[...] = mid
        if has_row:
            refs[2][...] = b[trace:]


def depth_kernel(tick, trace, columns, moving, has_row, level_ref, parity_ref, more_ref, both_ref, s_ref, given_ref, *refs):
    refs = list(refs)
    xs = [refs.pop(0) for _ in range(2)] if moving else [None] * 2
    z_in = refs.pop(0) if moving else None
    ys = [refs.pop(0) for _ in range(2)] if moving and has_row else [None] * 2
    mids = [refs.pop(0) for _ in range(2)]
    z_out = refs[0]
    width = z_out.shape[1]

    @pl.when(jnp.logical_and(level_ref[0] == tick, more_ref[0] == 1))
    def _():
        rows = slice(2 * trace, 3 * trace)

        def side_by_side(parts):
            return None if parts[0] is None else jnp.concatenate(parts, axis=1)

        pairs = [halves(ref, trace) + paired(z_in, trace, slot) for slot, ref in enumerate(xs)]
        xa, xb, za, zb = [side_by_side(parts) for parts in zip(*pairs)]
        ya = side_by_side([None if ref is None else ref[...] for ref in ys])
        mid = side_by_side([ref[...] for ref in mids])
        sa, sb = pair_sources(parity_ref, s_ref, given_ref, rows, columns)
        a = lower_side(both_ref.at[0], rows, trace, sa, (xa, ya, za)).astype(bf16)
        b = lower_side(both_ref.at[1], rows, trace, sb, (xb, mid, zb)).astype(bf16)
        for slot in range(2):
            part = slice(slot * width, (slot + 1) * width)
            z_out[2 * slot * trace : (2 * slot + 1) * trace, :] = a[:, part]
            z_out[(2 * slot + 1) * trace : (2 * slot + 2) * trace, :] = b[:, part]


def last_kernel(top, trace, width, base, has_row, level_ref, parity_ref, both_ref, s_ref, given_ref, turn_ref, *refs):
    del turn_ref
    refs = list(refs)
    own_ref, give_ref = refs[-2:]
    even = parity_ref[0] == 0
    zero = jnp.zeros((trace, width), bf16)

    def put(n, slot, a, b):
        rows = slice(n * trace, (n + 1) * trace)
        cols = slice(slot * width, (slot + 1) * width)
        own_ref[rows, cols] = jnp.where(even, a, b)
        give_ref[rows, cols] = jnp.where(even, b, a)

    for tick in range(top + 1):
        z_in = refs.pop(0) if tick else None
        xs = [refs.pop(0) for _ in range(2)] if tick else [None] * 2
        ys = [refs.pop(0) for _ in range(2)] if tick and has_row else [None] * 2
        mids = [refs.pop(0) for _ in range(2)] if tick < top else [None] * 2

        @pl.when(level_ref[0] == tick)
        def _():
            for slot in range(2):
                xa, xb = halves(xs[slot], trace)
                za, zb = paired(z_in, trace, slot)
                ya = None if ys[slot] is None else ys[slot][...]
                if mids[slot] is None:
                    rows = slice(trace, 2 * trace)
                    start = base + slot * width
                    sa, _ = pair_sources(parity_ref, s_ref, given_ref, rows, slice(start, start + width))
                    yb = lower_side(both_ref.at[0], rows, trace, sa, (xa, ya, za)).astype(bf16)
                else:
                    yb = mids[slot][...]
                put(0, slot, zero if xa is None else xa, zero if xb is None else xb)
                put(1, slot, zero if ya is None else ya, yb)
                put(2, slot, zero if za is None else za, zero if zb is None else zb)


def solved(columns, op_ref, r_ref, in_ref, start=0, stop=None):
    rows = in_ref.shape[0]
    stop = r_ref.shape[0] if stop is None else stop
    return (r_ref[start:stop, columns] + dot(op_ref[rows + start : rows + stop, :rows], in_ref[...])).astype(bf16)


def solve_kernel(half, base, side, parity_ref, op_ref, r_ref, in_ref, turn_ref, out_ref, token_ref):
    del turn_ref
    at = parity_ref[0] if side == 0 else 1 - parity_ref[0]
    columns = pl.ds(pl.multiple_of(at * half + base, 128), out_ref.shape[1])
    token_ref[...] = jnp.zeros(token_ref.shape, token_ref.dtype)
    out_ref[...] = solved(columns, op_ref, r_ref, in_ref)


def final_kernel(half, parity_ref, op_ref, r_ref, in_ref, turn_ref, *refs):
    del turn_ref
    *pieces, out_ref, buf, sems = refs
    width = in_ref.shape[1]
    blocks = sems.shape[0]
    step = buf.shape[0] // blocks

    def columns(n):
        at = parity_ref[0] if n % 2 == 0 else 1 - parity_ref[0]
        return pl.ds(pl.multiple_of(at * half + n // 2 * width, 128), width)

    copies = []
    for n in range(blocks):
        part = slice(n * step, (n + 1) * step)
        last = columns(len(pieces))
        buf[part, last] = solved(last, op_ref, r_ref, in_ref, n * step, (n + 1) * step)
        for k, piece in enumerate(pieces):
            buf[part, columns(k)] = piece[part, :]
        rows = pl.ds(n * step, step)
        copies.append(pltpu.make_async_copy(buf.at[rows, :], out_ref.at[rows, :], sems.at[n]))
        copies[-1].start()
    for copy in copies:
        copy.wait()


def shards(sizes, operator, sources):
    op = operator[0, 0, 0]
    src = sources[0, 0, 0]
    inner, columns = src.shape
    trace = (op.shape[0] - inner) // 3
    rows = 3 * trace
    half = columns // 2
    width = half // STREAMS
    nd, nx, ny = sizes
    top = nd + nx + ny // 2 - 3
    has_row = ny > 2
    row = lax.axis_index("gy")
    level = lax.axis_index("depth") + lax.axis_index("gx") + (row >> 1)
    level = level.astype(jnp.int32).reshape(1)
    parity = (row & 1).astype(jnp.int32).reshape(1)
    more = (lax.axis_index("depth") < nd - 1).astype(jnp.int32).reshape(1)
    op, src, level, parity, more = lax.optimization_barrier((op, src, level, parity, more))
    swap = [(j, j ^ 1) for j in range(ny)]

    upper = op[:rows]
    mid, rest = call(
        functools.partial(fetch_kernel, trace), [VMEM] * 2,
        [shaped((rows, trace)), shaped((rows, 2 * trace))], [VMEM] * 2, 4, 0, 0,
    )(upper, src)
    mid_got = lax.ppermute(mid, "gy", swap)
    give = call(
        functools.partial(give_kernel, half), [SMEM] + [VMEM] * 3, shaped((rows, half)), VMEM, 4, 0, 0
    )(parity, upper, src, mid)
    given = lax.ppermute(give, "gy", swap)
    rest_got = lax.ppermute(rest, "gy", swap)
    s = call(
        functools.partial(half_kernel, half), [SMEM] + [VMEM] * 3, shaped((rows, half), f32), VMEM, 4, 0, 0
    )(parity, upper, src, give)

    def joined(after, *parts):
        return call(both_kernel, [SMEM] + [VMEM] * (3 + len(parts)), shaped((2, rows, rows)), VMEM, 4, 0, 0)(
            parity, upper, mid_got, after, *parts
        )

    both = joined(s)
    turn = given
    xs = [[] for _ in range(STREAMS)]
    ys = [[] for _ in range(STREAMS)]
    zs = [[] for _ in range(STREAMS // 2)]
    mids = [[] for _ in range(STREAMS)]
    for tick in range(top):
        for n in range(STREAMS):
            slot = n % 2
            cols = slice(n * width, (n + 1) * width)
            outs = [shaped((2 * trace, width)), shaped((trace, width))] + [shaped((trace, width))] * has_row
            ins = [turn]
            if tick:
                ins += [xs[n][-1], zs[n // 2][tick - 1]] + ([ys[n][-1]] if has_row else [])
            sent = call(
                functools.partial(tick_kernel, tick, trace, cols, slot, tick > 0, has_row),
                [SMEM] * 2 + [VMEM] * (3 + len(ins)), outs, [VMEM] * len(outs), 4, 0, 0,
            )(level, parity, both, s, given, *ins)
            turn = sent[1]
            mids[n].append(turn)
            xs[n].append(lax.ppermute(sent[0], AXES, route(sizes, 1, tick)))
            if has_row:
                ys[n].append(lax.ppermute(sent[2], AXES, route(sizes, 2, tick)))
            if slot:
                both_slots = (n - 1, n)
                ins = []
                if tick:
                    ins += [xs[m][tick - 1] for m in both_slots] + [zs[n // 2][tick - 1]]
                    ins += [ys[m][tick - 1] for m in both_slots] if has_row else []
                ins += [mids[m][tick] for m in both_slots]
                cols = slice((n - 1) * width, (n + 1) * width)
                turn = call(
                    functools.partial(depth_kernel, tick, trace, cols, tick > 0, has_row),
                    [SMEM] * 3 + [VMEM] * (3 + len(ins)), shaped((4 * trace, width)), VMEM, 4, 0, 0,
                )(level, parity, more, both, s, given, *ins)
                zs[n // 2].append(lax.ppermute(turn, AXES, route(sizes, 0, tick)))
        if tick == 0:
            both = turn = joined(turn, rest_got)
        if tick == top // 2:
            r, turn = call(
                functools.partial(lower_kernel, rows), [VMEM] * 3,
                [shaped((inner, columns), f32), shaped((8, 128), f32)], [VMEM] * 2, 4, 0, 0,
            )(op, src, turn)
    pieces = []
    for p in range(STREAMS // 2):
        ins = []
        for tick in range(top + 1):
            ins += [zs[p][tick - 1]] if tick else []
            for part in (xs, ys) if has_row else (xs,):
                ins += [part[2 * p + slot][tick - 1] for slot in range(2)] if tick else []
            ins += [mids[2 * p + slot][tick] for slot in range(2)] if tick < top else []
        base = 2 * p * width
        mine, other = call(
            functools.partial(last_kernel, top, trace, width, base, has_row),
            [SMEM] * 2 + [VMEM] * (4 + len(ins)), [shaped((rows, 2 * width))] * 2, [VMEM] * 2, 4, 0, 0,
        )(level, parity, both, s, given, turn, *ins)
        back = lax.ppermute(other, "gy", swap)
        turn = mine
        for side, part in enumerate((mine, back)):
            if len(pieces) == STREAMS - 1:
                out = call(
                    functools.partial(final_kernel, half), [SMEM] + [VMEM] * (4 + len(pieces)),
                    shaped((inner, columns)), HBM, 6, 0, 0,
                    scratch=[pltpu.VMEM((inner, columns), bf16), pltpu.SemaphoreType.DMA((BLOCKS,))],
                )(parity, op, r, part, turn, *pieces)
            else:
                piece, turn = call(
                    functools.partial(solve_kernel, half, base, side), [SMEM] + [VMEM] * 4,
                    [shaped((inner, 2 * width)), shaped((8, 128), f32)], [VMEM] * 2, 4, 0, 0,
                )(parity, op, r, part, turn)
                pieces.append(piece)
    return out[None, None, None]


def solution(mesh):
    spec = P("depth", "gx", "gy", None, None)
    sizes = tuple(mesh.shape[a] for a in AXES)
    return jax.shard_map(
        functools.partial(shards, sizes), mesh=mesh, in_specs=(spec, spec), out_specs=spec, check_vma=False
    )
```

```python
import functools
import jax
import jax.numpy as jnp
from jax import lax
from jax.experimental import pallas as pl
from jax.experimental.pallas import tpu as pltpu
from jax.sharding import PartitionSpec as P

STREAMS = 4
BLOCKS = 2
REPEAT = (8, (5, 4, 4, 4), 4)
VMEM = pl.BlockSpec(memory_space=pltpu.VMEM)
SMEM = pl.BlockSpec(memory_space=pltpu.SMEM)
HBM = pl.BlockSpec(memory_space=pltpu.HBM)
AXES = ("depth", "gx", "gy")
f32 = jnp.float32
bf16 = jnp.bfloat16


def dot(a, b):
    return jnp.dot(a, b, preferred_element_type=f32)


def shaped(shape, dtype=bf16):
    return jax.ShapeDtypeStruct(shape, dtype)


def call(kernel, ins, outs, out_specs, mib, flops, nbytes, scratch=(), aliases=None):
    return pl.pallas_call(
        kernel,
        out_shape=outs,
        in_specs=ins,
        out_specs=out_specs,
        scratch_shapes=list(scratch),
        input_output_aliases=aliases or {},
        compiler_params=pltpu.CompilerParams(vmem_limit_bytes=mib << 20),
        cost_estimate=pl.CostEstimate(flops=flops, bytes_accessed=nbytes, transcendentals=0),
    )


def route(sizes, axis, tick, repeat):
    nd, nx, ny = sizes
    pairs = []
    for d in range(nd):
        for i in range(nx):
            for j in range(ny):
                group = j // 2
                at, to = [d, i, group], [d, i, group]
                to[axis] += 1
                if to[axis] < (nd, nx, ny // 2)[axis] and (sum(at) - tick) % repeat == 0:
                    end = (to[0] * nx + to[1]) * ny + 2 * to[2] + j % 2
                    pairs.append(((d * nx + i) * ny + j, end))
    return pairs


def fetch_kernel(trace, op_ref, turn_ref, mid_ref, rest_ref):
    del turn_ref
    mid_ref[...] = op_ref[:, trace : 2 * trace]
    rest_ref[:, :trace] = op_ref[:, :trace]
    rest_ref[:, trace:] = op_ref[:, 2 * trace : 3 * trace]


def give_kernel(half, parity_ref, op_ref, src_ref, turn_ref, give_ref):
    del turn_ref
    columns = pl.ds(pl.multiple_of((1 - parity_ref[0]) * half, 128), half)
    rows = op_ref.shape[0]
    give_ref[...] = dot(op_ref[:, rows:], src_ref[:, columns]).astype(bf16)


def half_kernel(half, parity_ref, op_ref, src_ref, turn_ref, out_ref):
    del turn_ref
    columns = pl.ds(pl.multiple_of(parity_ref[0] * half, 128), half)
    rows = out_ref.shape[0]
    step = rows // 3

    def body(n, _):
        part = pl.ds(pl.multiple_of(n * step, step), step)
        out_ref[part, :] = dot(op_ref[part, rows:], src_ref[:, columns])
        return 0

    lax.fori_loop(0, 3, body, 0)


def both_kernel(parity_ref, op_ref, mid_ref, turn_ref, *refs):
    del turn_ref
    *rest, both_ref = refs
    trace = mid_ref.shape[1]
    own, other = parity_ref[0], 1 - parity_ref[0]
    both_ref[own, :, trace : 2 * trace] = op_ref[:, trace : 2 * trace]
    both_ref[other, :, trace : 2 * trace] = mid_ref[...]
    for rest_ref in rest:
        both_ref[own, :, :trace] = op_ref[:, :trace]
        both_ref[own, :, 2 * trace :] = op_ref[:, 2 * trace : 3 * trace]
        both_ref[other, :, :trace] = rest_ref[:, :trace]
        both_ref[other, :, 2 * trace :] = rest_ref[:, trace:]


def lower_kernel(rows, op_ref, src_ref, turn_ref, r_ref, token_ref):
    del turn_ref
    step = r_ref.shape[0] // 3
    token_ref[...] = jnp.zeros(token_ref.shape, token_ref.dtype)

    def body(n, _):
        part = pl.ds(pl.multiple_of(n * step, step), step)
        below = pl.ds(pl.multiple_of(rows + n * step, step), step)
        r_ref[part, :] = dot(op_ref[below, rows:], src_ref[...])
        return 0

    lax.fori_loop(0, 3, body, 0)


def pair_sources(parity_ref, s_ref, given_ref, rows, columns):
    own, given = s_ref[rows, columns], given_ref[rows, columns].astype(f32)
    even = parity_ref[0] == 0
    return jnp.where(even, own, given), jnp.where(even, given, own)


def lower_side(op, rows, trace, total, parts):
    for n, part in enumerate(parts):
        if part is not None:
            total += dot(op[rows, n * trace : (n + 1) * trace], part)
    return total


def halves(ref, trace):
    return (None, None) if ref is None else (ref[:trace, :], ref[trace:, :])


def paired(ref, trace, slot):
    if ref is None:
        return None, None
    at = 2 * slot * trace
    return ref[at : at + trace, :], ref[at + trace : at + 2 * trace, :]


def tick_kernel(tick, trace, columns, slot, moving, has_row, level_ref, parity_ref, both_ref, s_ref, given_ref, turn_ref, *refs):
    del turn_ref
    refs = list(refs)
    x_in = refs.pop(0) if moving else None
    z_in = refs.pop(0) if moving else None
    y_in = refs.pop(0) if moving and has_row else None
    x_out, mid_out = refs[:2]

    @pl.when(level_ref[0] == tick)
    def _():
        xa, xb = halves(x_in, trace)
        za, zb = paired(z_in, trace, slot)
        ya = None if y_in is None else y_in[...]
        upper = slice(0, 2 * trace)
        sa, sb = pair_sources(parity_ref, s_ref, given_ref, upper, columns)
        a = lower_side(both_ref.at[0], upper, trace, sa, (xa, ya, za)).astype(bf16)
        mid = a[trace:]
        wanted = slice(0, (1 + has_row) * trace)
        b = lower_side(both_ref.at[1], wanted, trace, sb[wanted], (xb, None, zb))
        b = lower_side(both_ref.at[1], wanted, trace, b, (None, mid, None)).astype(bf16)
        x_out[:trace, :] = a[:trace]
        x_out[trace:, :] = b[:trace]
        mid_out[...] = mid
        if has_row:
            refs[2][...] = b[trace:]


def depth_kernel(tick, trace, columns, moving, has_row, level_ref, parity_ref, more_ref, both_ref, s_ref, given_ref, *refs):
    refs = list(refs)
    xs = [refs.pop(0) for _ in range(2)] if moving else [None] * 2
    z_in = refs.pop(0) if moving else None
    ys = [refs.pop(0) for _ in range(2)] if moving and has_row else [None] * 2
    mids = [refs.pop(0) for _ in range(2)]
    z_out = refs[0]
    width = z_out.shape[1]

    @pl.when(jnp.logical_and(level_ref[0] == tick, more_ref[0] == 1))
    def _():
        rows = slice(2 * trace, 3 * trace)

        def side_by_side(parts):
            return None if parts[0] is None else jnp.concatenate(parts, axis=1)

        pairs = [halves(ref, trace) + paired(z_in, trace, slot) for slot, ref in enumerate(xs)]
        xa, xb, za, zb = [side_by_side(parts) for parts in zip(*pairs)]
        ya = side_by_side([None if ref is None else ref[...] for ref in ys])
        mid = side_by_side([ref[...] for ref in mids])
        sa, sb = pair_sources(parity_ref, s_ref, given_ref, rows, columns)
        a = lower_side(both_ref.at[0], rows, trace, sa, (xa, ya, za)).astype(bf16)
        b = lower_side(both_ref.at[1], rows, trace, sb, (xb, mid, zb)).astype(bf16)
        for slot in range(2):
            part = slice(slot * width, (slot + 1) * width)
            z_out[2 * slot * trace : (2 * slot + 1) * trace, :] = a[:, part]
            z_out[(2 * slot + 1) * trace : (2 * slot + 2) * trace, :] = b[:, part]


def last_kernel(top, trace, width, base, has_row, level_ref, parity_ref, both_ref, s_ref, given_ref, turn_ref, *refs):
    del turn_ref
    refs = list(refs)
    own_ref, give_ref = refs[-2:]
    even = parity_ref[0] == 0
    zero = jnp.zeros((trace, width), bf16)

    def put(n, slot, a, b):
        rows = slice(n * trace, (n + 1) * trace)
        cols = slice(slot * width, (slot + 1) * width)
        own_ref[rows, cols] = jnp.where(even, a, b)
        give_ref[rows, cols] = jnp.where(even, b, a)

    for tick in range(top + 1):
        z_in = refs.pop(0) if tick else None
        xs = [refs.pop(0) for _ in range(2)] if tick else [None] * 2
        ys = [refs.pop(0) for _ in range(2)] if tick and has_row else [None] * 2
        mids = [refs.pop(0) for _ in range(2)] if tick < top else [None] * 2

        @pl.when(level_ref[0] == tick)
        def _():
            for slot in range(2):
                xa, xb = halves(xs[slot], trace)
                za, zb = paired(z_in, trace, slot)
                ya = None if ys[slot] is None else ys[slot][...]
                if mids[slot] is None:
                    rows = slice(trace, 2 * trace)
                    start = base + slot * width
                    sa, _ = pair_sources(parity_ref, s_ref, given_ref, rows, slice(start, start + width))
                    yb = lower_side(both_ref.at[0], rows, trace, sa, (xa, ya, za)).astype(bf16)
                else:
                    yb = mids[slot][...]
                put(0, slot, zero if xa is None else xa, zero if xb is None else xb)
                put(1, slot, zero if ya is None else ya, yb)
                put(2, slot, zero if za is None else za, zero if zb is None else zb)


def solved(columns, op_ref, r_ref, in_ref, start=0, stop=None):
    rows = in_ref.shape[0]
    stop = r_ref.shape[0] if stop is None else stop
    return (r_ref[start:stop, columns] + dot(op_ref[rows + start : rows + stop, :rows], in_ref[...])).astype(bf16)


def solve_kernel(half, base, side, parity_ref, op_ref, r_ref, in_ref, turn_ref, out_ref, token_ref):
    del turn_ref
    at = parity_ref[0] if side == 0 else 1 - parity_ref[0]
    columns = pl.ds(pl.multiple_of(at * half + base, 128), out_ref.shape[1])
    token_ref[...] = jnp.zeros(token_ref.shape, token_ref.dtype)
    out_ref[...] = solved(columns, op_ref, r_ref, in_ref)


def final_kernel(half, parity_ref, op_ref, r_ref, in_ref, turn_ref, *refs):
    del turn_ref
    *pieces, out_ref, buf, sems = refs
    width = in_ref.shape[1]
    blocks = sems.shape[0]
    step = buf.shape[0] // blocks

    def columns(n):
        at = parity_ref[0] if n % 2 == 0 else 1 - parity_ref[0]
        return pl.ds(pl.multiple_of(at * half + n // 2 * width, 128), width)

    copies = []
    for n in range(blocks):
        part = slice(n * step, (n + 1) * step)
        last = columns(len(pieces))
        buf[part, last] = solved(last, op_ref, r_ref, in_ref, n * step, (n + 1) * step)
        for k, piece in enumerate(pieces):
            buf[part, columns(k)] = piece[part, :]
        rows = pl.ds(n * step, step)
        copies.append(pltpu.make_async_copy(buf.at[rows, :], out_ref.at[rows, :], sems.at[n]))
        copies[-1].start()
    for copy in copies:
        copy.wait()


def shards(sizes, operator, sources):
    op = operator[0, 0, 0]
    src = sources[0, 0, 0]
    inner, columns = src.shape
    trace = (op.shape[0] - inner) // 3
    rows = 3 * trace
    half = columns // 2
    width = half // STREAMS
    nd, nx, ny = sizes
    top = nd + nx + ny // 2 - 3
    has_row = ny > 2
    row = lax.axis_index("gy")
    level = lax.axis_index("depth") + lax.axis_index("gx") + (row >> 1)
    level = level.astype(jnp.int32).reshape(1)
    parity = (row & 1).astype(jnp.int32).reshape(1)
    more = (lax.axis_index("depth") < nd - 1).astype(jnp.int32).reshape(1)
    op, src, level, parity, more = lax.optimization_barrier((op, src, level, parity, more))
    swap = [(j, j ^ 1) for j in range(ny)]

    upper = op[:rows]
    mid, rest = call(
        functools.partial(fetch_kernel, trace), [VMEM] * 2,
        [shaped((rows, trace)), shaped((rows, 2 * trace))], [VMEM] * 2, 4, 0, 0,
    )(upper, src)
    mid_got = lax.ppermute(mid, "gy", swap)
    give = call(
        functools.partial(give_kernel, half), [SMEM] + [VMEM] * 3, shaped((rows, half)), VMEM, 4, 0, 0
    )(parity, upper, src, mid)
    given = lax.ppermute(give, "gy", swap)
    rest_got = lax.ppermute(rest, "gy", swap)
    s = call(
        functools.partial(half_kernel, half), [SMEM] + [VMEM] * 3, shaped((rows, half), f32), VMEM, 4, 0, 0
    )(parity, upper, src, give)

    def joined(after, *parts):
        return call(both_kernel, [SMEM] + [VMEM] * (3 + len(parts)), shaped((2, rows, rows)), VMEM, 4, 0, 0)(
            parity, upper, mid_got, after, *parts
        )

    both = joined(s)
    turn = given
    xs = [[] for _ in range(STREAMS)]
    ys = [[] for _ in range(STREAMS)]
    zs = [[] for _ in range(STREAMS // 2)]
    mids = [[] for _ in range(STREAMS)]
    for tick in range(top):
        for n in range(STREAMS):
            slot = n % 2
            cols = slice(n * width, (n + 1) * width)
            outs = [shaped((2 * trace, width)), shaped((trace, width))] + [shaped((trace, width))] * has_row
            ins = [turn]
            if tick:
                ins += [xs[n][-1], zs[n // 2][tick - 1]] + ([ys[n][-1]] if has_row else [])
            sent = call(
                functools.partial(tick_kernel, tick, trace, cols, slot, tick > 0, has_row),
                [SMEM] * 2 + [VMEM] * (3 + len(ins)), outs, [VMEM] * len(outs), 4, 0, 0,
            )(level, parity, both, s, given, *ins)
            turn = sent[1]
            mids[n].append(turn)
            xs[n].append(lax.ppermute(sent[0], AXES, route(sizes, 1, tick, REPEAT[1][n])))
            if has_row:
                ys[n].append(lax.ppermute(sent[2], AXES, route(sizes, 2, tick, REPEAT[2])))
            if slot:
                both_slots = (n - 1, n)
                ins = []
                if tick:
                    ins += [xs[m][tick - 1] for m in both_slots] + [zs[n // 2][tick - 1]]
                    ins += [ys[m][tick - 1] for m in both_slots] if has_row else []
                ins += [mids[m][tick] for m in both_slots]
                cols = slice((n - 1) * width, (n + 1) * width)
                turn = call(
                    functools.partial(depth_kernel, tick, trace, cols, tick > 0, has_row),
                    [SMEM] * 3 + [VMEM] * (3 + len(ins)), shaped((4 * trace, width)), VMEM, 4, 0, 0,
                )(level, parity, more, both, s, given, *ins)
                zs[n // 2].append(lax.ppermute(turn, AXES, route(sizes, 0, tick, REPEAT[0])))
        if tick == 0:
            both = turn = joined(turn, rest_got)
        if tick == top // 2:
            r, turn = call(
                functools.partial(lower_kernel, rows), [VMEM] * 3,
                [shaped((inner, columns), f32), shaped((8, 128), f32)], [VMEM] * 2, 4, 0, 0,
            )(op, src, turn)
    pieces = []
    for p in range(STREAMS // 2):
        ins = []
        for tick in range(top + 1):
            ins += [zs[p][tick - 1]] if tick else []
            for part in (xs, ys) if has_row else (xs,):
                ins += [part[2 * p + slot][tick - 1] for slot in range(2)] if tick else []
            ins += [mids[2 * p + slot][tick] for slot in range(2)] if tick < top else []
        base = 2 * p * width
        mine, other = call(
            functools.partial(last_kernel, top, trace, width, base, has_row),
            [SMEM] * 2 + [VMEM] * (4 + len(ins)), [shaped((rows, 2 * width))] * 2, [VMEM] * 2, 4, 0, 0,
        )(level, parity, both, s, given, turn, *ins)
        back = lax.ppermute(other, "gy", swap)
        turn = mine
        for side, part in enumerate((mine, back)):
            if len(pieces) == STREAMS - 1:
                out = call(
                    functools.partial(final_kernel, half), [SMEM] + [VMEM] * (4 + len(pieces)),
                    shaped((inner, columns)), HBM, 6, 0, 0,
                    scratch=[pltpu.VMEM((inner, columns), bf16), pltpu.SemaphoreType.DMA((BLOCKS,))],
                )(parity, op, r, part, turn, *pieces)
            else:
                piece, turn = call(
                    functools.partial(solve_kernel, half, base, side), [SMEM] + [VMEM] * 4,
                    [shaped((inner, 2 * width)), shaped((8, 128), f32)], [VMEM] * 2, 4, 0, 0,
                )(parity, op, r, part, turn)
                pieces.append(piece)
    return out[None, None, None]


def solution(mesh):
    spec = P("depth", "gx", "gy", None, None)
    sizes = tuple(mesh.shape[a] for a in AXES)
    return jax.shard_map(
        functools.partial(shards, sizes), mesh=mesh, in_specs=(spec, spec), out_specs=spec, check_vma=False
    )
```

```python
import functools
import jax
import jax.numpy as jnp
from jax import lax
from jax.experimental import pallas as pl
from jax.experimental.pallas import tpu as pltpu
from jax.sharding import PartitionSpec as P

STREAMS = 4
BLOCKS = 2
REPEAT = (8, (5, 4, 4, 4), 4)
VMEM = pl.BlockSpec(memory_space=pltpu.VMEM)
SMEM = pl.BlockSpec(memory_space=pltpu.SMEM)
HBM = pl.BlockSpec(memory_space=pltpu.HBM)
AXES = ("depth", "gx", "gy")
f32 = jnp.float32
bf16 = jnp.bfloat16


def dot(a, b):
    return jnp.dot(a, b, preferred_element_type=f32)


def shaped(shape, dtype=bf16):
    return jax.ShapeDtypeStruct(shape, dtype)


def call(kernel, ins, outs, out_specs, mib, flops, nbytes, scratch=(), aliases=None):
    return pl.pallas_call(
        kernel,
        out_shape=outs,
        in_specs=ins,
        out_specs=out_specs,
        scratch_shapes=list(scratch),
        input_output_aliases=aliases or {},
        compiler_params=pltpu.CompilerParams(vmem_limit_bytes=mib << 20),
        cost_estimate=pl.CostEstimate(flops=flops, bytes_accessed=nbytes, transcendentals=0),
    )


def route(sizes, axis, tick, repeat):
    nd, nx, ny = sizes
    pairs = []
    for d in range(nd):
        for i in range(nx):
            for j in range(ny):
                group = j // 2
                at, to = [d, i, group], [d, i, group]
                to[axis] += 1
                if to[axis] < (nd, nx, ny // 2)[axis] and (sum(at) - tick) % repeat == 0:
                    end = (to[0] * nx + to[1]) * ny + 2 * to[2] + j % 2
                    pairs.append(((d * nx + i) * ny + j, end))
    return pairs


def fetch_kernel(trace, op_ref, turn_ref, mid_ref, rest_ref):
    del turn_ref
    mid_ref[...] = op_ref[:, trace : 2 * trace]
    rest_ref[:, :trace] = op_ref[:, :trace]
    rest_ref[:, trace:] = op_ref[:, 2 * trace : 3 * trace]


def give_kernel(half, parity_ref, op_ref, src_ref, turn_ref, give_ref):
    del turn_ref
    columns = pl.ds(pl.multiple_of((1 - parity_ref[0]) * half, 128), half)
    rows = op_ref.shape[0]
    give_ref[...] = dot(op_ref[:, rows:], src_ref[:, columns]).astype(bf16)


def half_kernel(half, parity_ref, op_ref, src_ref, turn_ref, out_ref):
    del turn_ref
    columns = pl.ds(pl.multiple_of(parity_ref[0] * half, 128), half)
    rows = out_ref.shape[0]
    step = rows // 3

    def body(n, _):
        part = pl.ds(pl.multiple_of(n * step, step), step)
        out_ref[part, :] = dot(op_ref[part, rows:], src_ref[:, columns])
        return 0

    lax.fori_loop(0, 3, body, 0)


def both_kernel(parity_ref, op_ref, mid_ref, turn_ref, *refs):
    del turn_ref
    *rest, both_ref = refs
    trace = mid_ref.shape[1]
    own, other = parity_ref[0], 1 - parity_ref[0]
    both_ref[own, :, trace : 2 * trace] = op_ref[:, trace : 2 * trace]
    both_ref[other, :, trace : 2 * trace] = mid_ref[...]
    for rest_ref in rest:
        both_ref[own, :, :trace] = op_ref[:, :trace]
        both_ref[own, :, 2 * trace :] = op_ref[:, 2 * trace : 3 * trace]
        both_ref[other, :, :trace] = rest_ref[:, :trace]
        both_ref[other, :, 2 * trace :] = rest_ref[:, trace:]


def lower_kernel(rows, op_ref, src_ref, turn_ref, r_ref, token_ref):
    del turn_ref
    step = r_ref.shape[0] // 3
    token_ref[...] = jnp.zeros(token_ref.shape, token_ref.dtype)

    def body(n, _):
        part = pl.ds(pl.multiple_of(n * step, step), step)
        below = pl.ds(pl.multiple_of(rows + n * step, step), step)
        r_ref[part, :] = dot(op_ref[below, rows:], src_ref[...])
        return 0

    lax.fori_loop(0, 3, body, 0)


def pair_sources(parity_ref, s_ref, given_ref, rows, columns):
    own, given = s_ref[rows, columns], given_ref[rows, columns].astype(f32)
    even = parity_ref[0] == 0
    return jnp.where(even, own, given), jnp.where(even, given, own)


def lower_side(op, rows, trace, total, parts):
    for n, part in enumerate(parts):
        if part is not None:
            total += dot(op[rows, n * trace : (n + 1) * trace], part)
    return total


def halves(ref, trace):
    return (None, None) if ref is None else (ref[:trace, :], ref[trace:, :])


def paired(ref, trace, slot):
    if ref is None:
        return None, None
    at = 2 * slot * trace
    return ref[at : at + trace, :], ref[at + trace : at + 2 * trace, :]


def tick_kernel(tick, trace, columns, slot, moving, has_row, level_ref, parity_ref, both_ref, s_ref, given_ref, turn_ref, *refs):
    del turn_ref
    refs = list(refs)
    x_in = refs.pop(0) if moving else None
    z_in = refs.pop(0) if moving else None
    y_in = refs.pop(0) if moving and has_row else None
    x_out, mid_out = refs[:2]

    @pl.when(level_ref[0] == tick)
    def _():
        xa, xb = halves(x_in, trace)
        za, zb = paired(z_in, trace, slot)
        ya = None if y_in is None else y_in[...]
        upper = slice(0, 2 * trace)
        wanted = slice(0, (1 + has_row) * trace)
        sa, _ = pair_sources(parity_ref, s_ref, given_ref, upper, columns)
        _, sb = pair_sources(parity_ref, s_ref, given_ref, wanted, columns)
        a = lower_side(both_ref.at[0], upper, trace, sa, (xa, ya, za)).astype(bf16)
        mid = a[trace:]
        b = lower_side(both_ref.at[1], wanted, trace, sb, (xb, None, zb))
        b = lower_side(both_ref.at[1], wanted, trace, b, (None, mid, None)).astype(bf16)
        x_out[:trace, :] = a[:trace]
        x_out[trace:, :] = b[:trace]
        mid_out[...] = mid
        if has_row:
            refs[2][...] = b[trace:]


def depth_kernel(tick, trace, columns, moving, has_row, level_ref, parity_ref, more_ref, both_ref, s_ref, given_ref, *refs):
    refs = list(refs)
    xs = [refs.pop(0) for _ in range(2)] if moving else [None] * 2
    z_in = refs.pop(0) if moving else None
    ys = [refs.pop(0) for _ in range(2)] if moving and has_row else [None] * 2
    mids = [refs.pop(0) for _ in range(2)]
    z_out = refs[0]
    width = z_out.shape[1]

    @pl.when(jnp.logical_and(level_ref[0] == tick, more_ref[0] == 1))
    def _():
        rows = slice(2 * trace, 3 * trace)

        def side_by_side(parts):
            return None if parts[0] is None else jnp.concatenate(parts, axis=1)

        pairs = [halves(ref, trace) + paired(z_in, trace, slot) for slot, ref in enumerate(xs)]
        xa, xb, za, zb = [side_by_side(parts) for parts in zip(*pairs)]
        ya = side_by_side([None if ref is None else ref[...] for ref in ys])
        mid = side_by_side([ref[...] for ref in mids])
        sa, sb = pair_sources(parity_ref, s_ref, given_ref, rows, columns)
        a = lower_side(both_ref.at[0], rows, trace, sa, (xa, ya, za)).astype(bf16)
        b = lower_side(both_ref.at[1], rows, trace, sb, (xb, mid, zb)).astype(bf16)
        for slot in range(2):
            part = slice(slot * width, (slot + 1) * width)
            z_out[2 * slot * trace : (2 * slot + 1) * trace, :] = a[:, part]
            z_out[(2 * slot + 1) * trace : (2 * slot + 2) * trace, :] = b[:, part]


def last_kernel(top, trace, width, base, has_row, level_ref, parity_ref, both_ref, s_ref, given_ref, turn_ref, *refs):
    del turn_ref
    refs = list(refs)
    own_ref, give_ref = refs[-2:]
    even = parity_ref[0] == 0
    zero = jnp.zeros((trace, width), bf16)

    def put(n, slot, a, b):
        rows = slice(n * trace, (n + 1) * trace)
        cols = slice(slot * width, (slot + 1) * width)
        own_ref[rows, cols] = jnp.where(even, a, b)
        give_ref[rows, cols] = jnp.where(even, b, a)

    for tick in range(top + 1):
        z_in = refs.pop(0) if tick else None
        xs = [refs.pop(0) for _ in range(2)] if tick else [None] * 2
        ys = [refs.pop(0) for _ in range(2)] if tick and has_row else [None] * 2
        mids = [refs.pop(0) for _ in range(2)] if tick < top else [None] * 2

        @pl.when(level_ref[0] == tick)
        def _():
            for slot in range(2):
                xa, xb = halves(xs[slot], trace)
                za, zb = paired(z_in, trace, slot)
                ya = None if ys[slot] is None else ys[slot][...]
                if mids[slot] is None:
                    rows = slice(trace, 2 * trace)
                    start = base + slot * width
                    sa, _ = pair_sources(parity_ref, s_ref, given_ref, rows, slice(start, start + width))
                    yb = lower_side(both_ref.at[0], rows, trace, sa, (xa, ya, za)).astype(bf16)
                else:
                    yb = mids[slot][...]
                put(0, slot, zero if xa is None else xa, zero if xb is None else xb)
                put(1, slot, zero if ya is None else ya, yb)
                put(2, slot, zero if za is None else za, zero if zb is None else zb)


def solved(columns, op_ref, r_ref, in_ref, start=0, stop=None):
    rows = in_ref.shape[0]
    stop = r_ref.shape[0] if stop is None else stop
    return (r_ref[start:stop, columns] + dot(op_ref[rows + start : rows + stop, :rows], in_ref[...])).astype(bf16)


def solve_kernel(half, base, side, parity_ref, op_ref, r_ref, in_ref, turn_ref, out_ref, token_ref):
    del turn_ref
    at = parity_ref[0] if side == 0 else 1 - parity_ref[0]
    columns = pl.ds(pl.multiple_of(at * half + base, 128), out_ref.shape[1])
    token_ref[...] = jnp.zeros(token_ref.shape, token_ref.dtype)
    out_ref[...] = solved(columns, op_ref, r_ref, in_ref)


def final_kernel(half, parity_ref, op_ref, r_ref, in_ref, turn_ref, *refs):
    del turn_ref
    *pieces, out_ref, buf, sems = refs
    width = in_ref.shape[1]
    blocks = sems.shape[0]
    step = buf.shape[0] // blocks

    def columns(n):
        at = parity_ref[0] if n % 2 == 0 else 1 - parity_ref[0]
        return pl.ds(pl.multiple_of(at * half + n // 2 * width, 128), width)

    copies = []
    for n in range(blocks):
        part = slice(n * step, (n + 1) * step)
        last = columns(len(pieces))
        buf[part, last] = solved(last, op_ref, r_ref, in_ref, n * step, (n + 1) * step)
        for k, piece in enumerate(pieces):
            buf[part, columns(k)] = piece[part, :]
        rows = pl.ds(n * step, step)
        copies.append(pltpu.make_async_copy(buf.at[rows, :], out_ref.at[rows, :], sems.at[n]))
        copies[-1].start()
    for copy in copies:
        copy.wait()


def shards(sizes, operator, sources):
    op = operator[0, 0, 0]
    src = sources[0, 0, 0]
    inner, columns = src.shape
    trace = (op.shape[0] - inner) // 3
    rows = 3 * trace
    half = columns // 2
    width = half // STREAMS
    nd, nx, ny = sizes
    top = nd + nx + ny // 2 - 3
    has_row = ny > 2
    row = lax.axis_index("gy")
    level = lax.axis_index("depth") + lax.axis_index("gx") + (row >> 1)
    level = level.astype(jnp.int32).reshape(1)
    parity = (row & 1).astype(jnp.int32).reshape(1)
    more = (lax.axis_index("depth") < nd - 1).astype(jnp.int32).reshape(1)
    op, src, level, parity, more = lax.optimization_barrier((op, src, level, parity, more))
    swap = [(j, j ^ 1) for j in range(ny)]

    upper = op[:rows]
    mid, rest = call(
        functools.partial(fetch_kernel, trace), [VMEM] * 2,
        [shaped((rows, trace)), shaped((rows, 2 * trace))], [VMEM] * 2, 4, 0, 0,
    )(upper, src)
    mid_got = lax.ppermute(mid, "gy", swap)
    give = call(
        functools.partial(give_kernel, half), [SMEM] + [VMEM] * 3, shaped((rows, half)), VMEM, 4, 0, 0
    )(parity, upper, src, mid)
    given = lax.ppermute(give, "gy", swap)
    rest_got = lax.ppermute(rest, "gy", swap)
    s = call(
        functools.partial(half_kernel, half), [SMEM] + [VMEM] * 3, shaped((rows, half), f32), VMEM, 4, 0, 0
    )(parity, upper, src, give)

    def joined(after, *parts):
        return call(both_kernel, [SMEM] + [VMEM] * (3 + len(parts)), shaped((2, rows, rows)), VMEM, 4, 0, 0)(
            parity, upper, mid_got, after, *parts
        )

    both = joined(s)
    turn = given
    xs = [[] for _ in range(STREAMS)]
    ys = [[] for _ in range(STREAMS)]
    zs = [[] for _ in range(STREAMS // 2)]
    mids = [[] for _ in range(STREAMS)]
    for tick in range(top):
        for n in range(STREAMS):
            slot = n % 2
            cols = slice(n * width, (n + 1) * width)
            outs = [shaped((2 * trace, width)), shaped((trace, width))] + [shaped((trace, width))] * has_row
            ins = [turn]
            if tick:
                ins += [xs[n][-1], zs[n // 2][tick - 1]] + ([ys[n][-1]] if has_row else [])
            sent = call(
                functools.partial(tick_kernel, tick, trace, cols, slot, tick > 0, has_row),
                [SMEM] * 2 + [VMEM] * (3 + len(ins)), outs, [VMEM] * len(outs), 4, 0, 0,
            )(level, parity, both, s, given, *ins)
            turn = sent[1]
            mids[n].append(turn)
            xs[n].append(lax.ppermute(sent[0], AXES, route(sizes, 1, tick, REPEAT[1][n])))
            if has_row:
                ys[n].append(lax.ppermute(sent[2], AXES, route(sizes, 2, tick, REPEAT[2])))
            if slot:
                both_slots = (n - 1, n)
                ins = []
                if tick:
                    ins += [xs[m][tick - 1] for m in both_slots] + [zs[n // 2][tick - 1]]
                    ins += [ys[m][tick - 1] for m in both_slots] if has_row else []
                ins += [mids[m][tick] for m in both_slots]
                cols = slice((n - 1) * width, (n + 1) * width)
                turn = call(
                    functools.partial(depth_kernel, tick, trace, cols, tick > 0, has_row),
                    [SMEM] * 3 + [VMEM] * (3 + len(ins)), shaped((4 * trace, width)), VMEM, 4, 0, 0,
                )(level, parity, more, both, s, given, *ins)
                zs[n // 2].append(lax.ppermute(turn, AXES, route(sizes, 0, tick, REPEAT[0])))
        if tick == 0:
            both = turn = joined(turn, rest_got)
        if tick == top // 2:
            r, turn = call(
                functools.partial(lower_kernel, rows), [VMEM] * 3,
                [shaped((inner, columns), f32), shaped((8, 128), f32)], [VMEM] * 2, 4, 0, 0,
            )(op, src, turn)
    pieces = []
    for p in range(STREAMS // 2):
        ins = []
        for tick in range(top + 1):
            ins += [zs[p][tick - 1]] if tick else []
            for part in (xs, ys) if has_row else (xs,):
                ins += [part[2 * p + slot][tick - 1] for slot in range(2)] if tick else []
            ins += [mids[2 * p + slot][tick] for slot in range(2)] if tick < top else []
        base = 2 * p * width
        mine, other = call(
            functools.partial(last_kernel, top, trace, width, base, has_row),
            [SMEM] * 2 + [VMEM] * (4 + len(ins)), [shaped((rows, 2 * width))] * 2, [VMEM] * 2, 4, 0, 0,
        )(level, parity, both, s, given, turn, *ins)
        back = lax.ppermute(other, "gy", swap)
        turn = mine
        for side, part in enumerate((mine, back)):
            if len(pieces) == STREAMS - 1:
                out = call(
                    functools.partial(final_kernel, half), [SMEM] + [VMEM] * (4 + len(pieces)),
                    shaped((inner, columns)), HBM, 6, 0, 0,
                    scratch=[pltpu.VMEM((inner, columns), bf16), pltpu.SemaphoreType.DMA((BLOCKS,))],
                )(parity, op, r, part, turn, *pieces)
            else:
                piece, turn = call(
                    functools.partial(solve_kernel, half, base, side), [SMEM] + [VMEM] * 4,
                    [shaped((inner, 2 * width)), shaped((8, 128), f32)], [VMEM] * 2, 4, 0, 0,
                )(parity, op, r, part, turn)
                pieces.append(piece)
    return out[None, None, None]


def solution(mesh):
    spec = P("depth", "gx", "gy", None, None)
    sizes = tuple(mesh.shape[a] for a in AXES)
    return jax.shard_map(
        functools.partial(shards, sizes), mesh=mesh, in_specs=(spec, spec), out_specs=spec, check_vma=False
    )
```
